32 devices in a mesh: mem: 8 (over z, core), pat: 4 (over y, x).
Axes of the slice: x: 2, y: 2, z: 4, core: 2. Of those that a mesh axis runs over, the one named last changes fastest.
Arguments:
- background_realisations: bfloat16 [256, 8, 4, 512], P('mem', None, 'pat'), may hold values from -6 to 6
- sensed_spreads: bfloat16 [8, 4, 512, 256], P('mem', 'pat'), may hold values from -33 to 33
- departure_vector: bfloat16 [8, 4, 512], P('mem', 'pat'), may hold values from -6 to 6
- measurement_weights: bfloat16 [8, 4, 512], P('mem', 'pat'), may hold values from 0.099609375 to 10
- adjacent_tile_labels: int32 [8, 4, 9], P('mem', 'pat'), may hold values from 0 to 8, as said below
- active_lengths: int32 [8, 4], P('mem', 'pat'), may hold values from 1 to 9, as said below
Outputs:
- analysis: bfloat16 [256, 8, 4, 512], P('mem', None, 'pat')
The draws below stay inside these ranges and needn't reach their ends.
Inputs may be any that keep to these rules, and one draw needn't show every extreme that they name: `adjacent_tile_labels`: in each patch's list the 9 codes are distinct; every code among the first active_lengths entries names a block inside the 8 patch rows. `active_lengths`: some patch uses all 9 blocks in every draw.
All inputs are finite; a program needn't handle non-finite values.
Results may differ from the reference program's by a relative error of at most 0.011.
Values may be sent and summed in bfloat16 or wider, within the bound.
A program may use at most 64 MiB of HBM per device.

```python
import math
import jax
import jax.numpy as jnp
from jax import lax

NUM_REALISATIONS = 256
NUM_READINGS = 512
NEIGH = 9
ITERS = 12
REGION_EXTENT = 512
REGION_TALL = 8
REGION_WIDE = 4


mode_strength = 3.1623


def neighbour_plan(key):
    code_list = jnp.arange(NEIGH, dtype=jnp.int32)
    shift_row = code_list // 3 - 1
    row_index = jnp.arange(REGION_TALL, dtype=jnp.int32)[:, None, None]
    outside = (row_index + shift_row[None, None, :] < 0) | (row_index + shift_row[None, None, :] >= REGION_TALL)
    outside = jnp.broadcast_to(outside, (REGION_TALL, REGION_WIDE, NEIGH)).astype(jnp.int32)
    scores = jax.random.randint(jax.random.fold_in(key, 101), (REGION_TALL, REGION_WIDE, NEIGH), 0, 4096) * 16 + code_list[None, None, :] + outside * 1000000
    ranked = jnp.argsort(scores, axis=-1).astype(jnp.int32)
    inside = NEIGH - jnp.sum(outside, axis=-1)
    light_load = jax.random.randint(jax.random.fold_in(key, 102), (REGION_TALL, REGION_WIDE), 1, 4)
    heavy_flag = jax.random.randint(jax.random.fold_in(key, 103), (REGION_TALL, REGION_WIDE), 0, 4)
    wanted = jnp.where(heavy_flag == 0, NEIGH, light_load)
    wanted = wanted.at[1, 0].set(NEIGH)
    return (ranked, jnp.minimum(wanted, inside).astype(jnp.int32))


def draw_adjacent_tile_labels(key, part):
    return neighbour_plan(key)[0]


def draw_active_lengths(key, part):
    return neighbour_plan(key)[1]


def draw_sensed_spreads(key, part):
    jitter_seed = jax.random.fold_in(key, 201)
    loading_key = jax.random.fold_in(key, 202)
    realisation_seed = jax.random.fold_in(key, 203)
    random_jitter = jnp.clip(jax.random.normal(jitter_seed, (REGION_TALL, REGION_WIDE, NUM_READINGS, NUM_REALISATIONS), jnp.float32), -4.0, 4.0)
    loading = jnp.clip(jax.random.normal(loading_key, (REGION_TALL, REGION_WIDE, NUM_READINGS, 1), jnp.float32), -3.0, 3.0)
    realisation_pattern = jnp.clip(jax.random.normal(realisation_seed, (NUM_REALISATIONS,), jnp.float32), -3.0, 3.0)
    return (random_jitter + mode_strength * loading * realisation_pattern[None, None, None, :]).astype(jnp.bfloat16)


def block_levels(stream_key, extent, shards, least, high):
    def one(position, shards_of):
        heights = jax.random.uniform(jax.random.fold_in(jax.random.fold_in(stream_key, 6), position), (shards_of,), jnp.float32, least / len(shards), high / len(shards))
        return jnp.repeat(jnp.exp(heights), extent[position] // shards_of).reshape((-1,) + (1,) * (len(extent) - position - 1))

    factor_of = one(*shards[0])
    for cut in shards[1:]:
        factor_of = factor_of * one(*cut)
    return factor_of


def noise(stream_key, extent, scale, bound, split=(), held_as=jnp.bfloat16):
    values = scale * jax.random.normal(stream_key, extent, jnp.float32)
    if split:
        values = values * block_levels(stream_key, extent, split, -0.22, 0.18)
    return jnp.clip(values, -bound, bound).astype(held_as)


def setup_inputs(seed: int = 0) -> dict:
    streams_of = jax.random.split(jax.random.key(seed), 7)
    background_realisations = noise(streams_of[0], (NUM_REALISATIONS, REGION_TALL, REGION_WIDE, REGION_EXTENT), 1.0, 6.0, ((0, 8), (2, 4)))
    sensed_spreads = draw_sensed_spreads(jax.random.fold_in(streams_of[6], 71), 0)
    departure_vector = noise(streams_of[2], (REGION_TALL, REGION_WIDE, NUM_READINGS), 1.0, 6.0, ((0, 8), (1, 4)))
    measurement_weights = jnp.clip(jnp.exp(math.log(10.0) - 4.609084 * jax.random.uniform(streams_of[3], (REGION_TALL, REGION_WIDE, NUM_READINGS), jnp.float32) ** block_levels(streams_of[3], (REGION_TALL, REGION_WIDE, NUM_READINGS), ((0, 8), (1, 4)), -0.2, 0.2)), 0.099609375, 10.0).astype(jnp.bfloat16)
    adjacent_tile_labels = draw_adjacent_tile_labels(jax.random.fold_in(streams_of[6], 71), 0)
    active_lengths = draw_active_lengths(jax.random.fold_in(streams_of[6], 71), 0)
    return dict(background_realisations=background_realisations, sensed_spreads=sensed_spreads, departure_vector=departure_vector, measurement_weights=measurement_weights, adjacent_tile_labels=adjacent_tile_labels, active_lengths=active_lengths)


def transform(gram, drive):
    trajectory_vectors = gram.shape[-1]
    identity = jnp.eye(trajectory_vectors, dtype=jnp.float32)
    system = (trajectory_vectors - 1.0) * identity + gram
    frobenius = jnp.sqrt(jnp.sum(system * system))
    iterate = system / frobenius
    inverse_root = identity
    for sweep in range(ITERS):
        correction = 1.5 * identity - 0.5 * jnp.dot(inverse_root, iterate, precision=lax.Precision.HIGHEST)
        iterate = jnp.dot(iterate, correction, precision=lax.Precision.HIGHEST)
        inverse_root = jnp.dot(correction, inverse_root, precision=lax.Precision.HIGHEST)
    spread_part = inverse_root * jnp.sqrt((trajectory_vectors - 1.0) / frobenius)
    inner = jnp.dot(inverse_root, drive, precision=lax.Precision.HIGHEST)
    mean_part = jnp.dot(inverse_root, inner, precision=lax.Precision.HIGHEST) / frobenius
    return spread_part + mean_part[:, None]

def analyse_patch(state_block, blocks, innov_rows, rinv_rows, taper_list):
    weight = rinv_rows.astype(jnp.float32) * taper_list[:, None]
    scaled = (blocks.astype(jnp.float32) * weight[:, :, None]).astype(jnp.bfloat16)
    weighted_innov = (weight * innov_rows.astype(jnp.float32)).astype(jnp.bfloat16)
    gram = jnp.einsum('nbk,nbl->kl', scaled.astype(jnp.float32), blocks.astype(jnp.float32), precision=lax.Precision.HIGHEST)
    drive = jnp.einsum('nb,nbk->k', weighted_innov.astype(jnp.float32), blocks.astype(jnp.float32), precision=lax.Precision.HIGHEST)
    mixing = transform(gram, drive).astype(jnp.bfloat16)
    values = state_block.astype(jnp.float32)
    center = lax.optimization_barrier(jnp.mean(values, axis=0))
    anomaly = (values - center[None, :]).astype(jnp.bfloat16)
    mixed = jnp.einsum('ks,ki->is', anomaly.astype(jnp.float32), mixing.astype(jnp.float32), precision=lax.Precision.HIGHEST)
    return (center[None, :] + mixed).astype(jnp.bfloat16)

def reference(background_realisations, sensed_spreads, departure_vector, measurement_weights, adjacent_tile_labels, active_lengths):
    row_index = jnp.arange(REGION_TALL, dtype=jnp.int32)[:, None, None]
    col_index = jnp.arange(REGION_WIDE, dtype=jnp.int32)[None, :, None]
    shift_row = (adjacent_tile_labels // 3 - 1).astype(jnp.int32)
    shift_col = (adjacent_tile_labels % 3 - 1).astype(jnp.int32)
    source_row = jnp.clip(row_index + shift_row, 0, REGION_TALL - 1)
    source_col = (col_index + shift_col) % REGION_WIDE
    source = (source_row * REGION_WIDE + source_col).astype(jnp.int32)
    slot_index = jnp.arange(NEIGH, dtype=jnp.int32)
    live = (slot_index[None, None, :] < active_lengths[:, :, None]).astype(jnp.float32)
    taper = jnp.exp(-0.5 * (shift_row * shift_row + shift_col * shift_col).astype(jnp.float32)) * live
    stacked_segments = sensed_spreads.reshape(REGION_TALL * REGION_WIDE, NUM_READINGS, NUM_REALISATIONS)
    flat_innov = departure_vector.reshape(REGION_TALL * REGION_WIDE, NUM_READINGS)
    flat_rinv = measurement_weights.reshape(REGION_TALL * REGION_WIDE, NUM_READINGS)
    tile_vectors = jnp.transpose(background_realisations, (1, 2, 0, 3))

    def patch_from(state_block, source_list, taper_list):
        return analyse_patch(state_block, stacked_segments[source_list], flat_innov[source_list], flat_rinv[source_list], taper_list)

    def one_row(inputs):
        row_states, row_source, row_taper = inputs
        return jax.vmap(patch_from)(row_states, row_source, row_taper)
    analysed = lax.map(one_row, (tile_vectors, source, taper))
    return jnp.transpose(analysed, (2, 0, 1, 3))
```

```python
import functools

import jax
import jax.numpy as jnp
from jax import lax
from jax.experimental import pallas as pl
from jax.experimental.pallas import tpu as pltpu
from jax.sharding import PartitionSpec as P

ITERS = 12


def split(value):
    high = value.astype(jnp.bfloat16)
    low = (value - high.astype(jnp.float32)).astype(jnp.bfloat16)
    return high, low


def product(left, right):
    return jnp.dot(
        jnp.concatenate([left[1], left[0], left[0]], axis=1),
        jnp.concatenate([right[0], right[1], right[0]], axis=0),
        preferred_element_type=jnp.float32,
    )


def kernel(
    rows,
    cols,
    states_ref,
    spreads_ref,
    innov_ref,
    rinv_ref,
    labels_ref,
    length_ref,
    out_ref,
    forecast,
    grams,
    coefs,
    sums,
    arrived,
    total,
    y_high,
    y_low,
    z_high,
    z_low,
    anomaly,
    analysed,
    fsend,
    frecv,
    gsend,
    grecv,
    ysend,
    yrecv,
    csend,
    crecv,
    ssend,
    srecv,
    osend,
    orecv,
):
    row = lax.axis_index("mem")
    col = lax.axis_index("pat")
    odd = lax.rem(col, 2)
    partner = col + 1 - 2 * odd
    onward = lax.rem(col + 2 - 4 * odd + cols, cols)
    behind = lax.rem(col - 2 + 4 * odd + cols, cols)
    members = forecast.shape[0] * forecast.shape[1]
    half = members // 2
    chunks = ((0, half), (half, half), (2 * half, half + 8))

    barrier = pltpu.get_barrier_semaphore()
    greeted = 0
    for step in range(1, rows):
        pl.semaphore_signal(barrier, 1, device_id={"mem": lax.rem(row + step, rows)})
        greeted += 1
    pat_peers = [partner, onward] + ([behind] if cols > 4 else [])
    for peer in pat_peers:
        pl.semaphore_signal(barrier, 1, device_id={"pat": peer})
        greeted += 1

    slot = lax.broadcasted_iota(jnp.int32, (16, labels_ref.shape[2]), 1)
    code = lax.broadcasted_iota(jnp.int32, (16, labels_ref.shape[2]), 0)
    used = (labels_ref[0] == code) & (slot < length_ref[...])
    shift_row = code // 3 - 1
    shift_col = code % 3 - 1
    distance = (shift_row * shift_row + shift_col * shift_col).astype(jnp.float32)
    coefficient = jnp.sum(
        jnp.where(used, jnp.exp(-0.5 * distance), 0.0), axis=1, keepdims=True
    )
    coefs[1] = jnp.broadcast_to(coefficient, coefs.shape[1:])

    block = spreads_ref[...]
    weight = rinv_ref[0].astype(jnp.float32)
    scaled = jnp.concatenate(split(block.astype(jnp.float32).T * weight), axis=1)
    twice = jnp.concatenate([block, block], axis=0)
    upper = jnp.dot(scaled[:half], twice, preferred_element_type=jnp.float32)
    lower = jnp.dot(scaled[half:], twice[:, half:], preferred_element_type=jnp.float32)
    grams[0, 0:half] = upper[:, :half]
    grams[0, half : 2 * half] = upper[:, half:]
    grams[0, 2 * half : 3 * half] = lower
    weighted = split(weight * innov_ref[0].astype(jnp.float32))
    drive = jnp.dot(
        jnp.broadcast_to(jnp.concatenate(weighted, axis=1), (16, 2 * weight.shape[1])),
        twice,
        preferred_element_type=jnp.float32,
    )
    grams[0, 3 * half : 3 * half + 8] = jnp.concatenate(
        [drive[0:4, :half], drive[0:4, half:]], axis=0
    )
    pl.semaphore_wait(barrier, greeted)

    def across(part):
        start, size = chunks[part]
        return pltpu.make_async_remote_copy(
            src_ref=grams.at[0, pl.ds(start, size)],
            dst_ref=grams.at[1, pl.ds(start, size)],
            send_sem=gsend.at[part],
            recv_sem=grecv.at[part],
            device_id={"pat": partner},
        )

    def relay(part):
        start, size = chunks[part]
        return pltpu.make_async_remote_copy(
            src_ref=grams.at[1, pl.ds(start, size)],
            dst_ref=grams.at[2, pl.ds(start, size)],
            send_sem=ysend.at[part],
            recv_sem=yrecv.at[part],
            device_id={"pat": onward},
        )

    def coef_copy(up):
        return pltpu.make_async_remote_copy(
            src_ref=coefs.at[1],
            dst_ref=coefs.at[0 if up else 2],
            send_sem=csend.at[0 if up else 1],
            recv_sem=crecv.at[0 if up else 1],
            device_id={"mem": row + 1 if up else row - 1},
        )

    def sum_copy(up, part):
        start, size = chunks[part]
        side = 0 if up else 1
        return pltpu.make_async_remote_copy(
            src_ref=sums.at[side, pl.ds(start, size)],
            dst_ref=arrived.at[side, pl.ds(start, size)],
            send_sem=ssend.at[side, part],
            recv_sem=srecv.at[side, part],
            device_id={"mem": row + 1 if up else row - 1},
        )

    def forecast_copy(step):
        peer = lax.rem(row + step, rows)
        return pltpu.make_async_remote_copy(
            src_ref=states_ref.at[peer],
            dst_ref=forecast.at[row],
            send_sem=fsend.at[step],
            recv_sem=frecv.at[step],
            device_id={"mem": peer},
        )

    def analysis_copy(step):
        peer = lax.rem(row + step, rows)
        return pltpu.make_async_remote_copy(
            src_ref=analysed.at[peer],
            dst_ref=out_ref.at[row],
            send_sem=osend.at[step],
            recv_sem=orecv.at[step],
            device_id={"mem": peer},
        )

    for part in range(3):
        across(part).start()

    @pl.when(row < rows - 1)
    def _():
        coef_copy(True).start()

    @pl.when(row > 0)
    def _():
        coef_copy(False).start()

    for step in range(1, rows):
        forecast_copy(step).start()
    forecast[row] = states_ref[row]

    for part in range(3):
        across(part).wait_recv()
        relay(part).start()

    @pl.when(row > 0)
    def _():
        coef_copy(True).wait_recv()

    @pl.when(row < rows - 1)
    def _():
        coef_copy(False).wait_recv()

    def combined(target, first, start, size):
        own = coefs[target, pl.ds(first + 1, 1), :]
        near = coefs[target, pl.ds(first + 2 - 2 * odd, 1), :]
        far = coefs[target, pl.ds(first + 2 * odd, 1), :]
        piece = pl.ds(start, size)
        return own * grams[0, piece] + near * grams[1, piece] + far * grams[2, piece]

    for part in range(3):
        relay(part).wait_recv()
        start, size = chunks[part]

        @pl.when(row < rows - 1)
        def _():
            sums[0, pl.ds(start, size)] = combined(2, 0, start, size)
            sum_copy(True, part).start()

        @pl.when(row > 0)
        def _():
            sums[1, pl.ds(start, size)] = combined(0, 6, start, size)
            sum_copy(False, part).start()

        total[pl.ds(start, size)] = combined(1, 3, start, size)

    for step in range(1, rows):
        forecast_copy(step).wait_recv()
    values = forecast[...].reshape(members, forecast.shape[2]).astype(jnp.float32)
    center = jnp.sum(values, axis=0, keepdims=True) * (1.0 / members)
    anomaly[...] = (values - center).astype(jnp.bfloat16)

    for part in range(3):
        start, size = chunks[part]

        @pl.when(row > 0)
        def _():
            sum_copy(True, part).wait_recv()
            total[pl.ds(start, size)] += arrived[0, pl.ds(start, size)]

        @pl.when(row < rows - 1)
        def _():
            sum_copy(False, part).wait_recv()
            total[pl.ds(start, size)] += arrived[1, pl.ds(start, size)]

    eye_half = (
        lax.broadcasted_iota(jnp.int32, (half, half), 0)
        == lax.broadcasted_iota(jnp.int32, (half, half), 1)
    ).astype(jnp.float32)
    first = total[0:half] + (members - 1.0) * eye_half
    cross = total[half : 2 * half]
    last = total[2 * half : 3 * half] + (members - 1.0) * eye_half
    squares = first * first + 2.0 * (cross * cross) + last * last
    frobenius = jnp.sqrt(
        jnp.sum(jnp.sum(squares, axis=0, keepdims=True), axis=1, keepdims=True)
    )
    system = jnp.concatenate(
        [
            jnp.concatenate([first, cross], axis=1),
            jnp.concatenate([cross.T, last], axis=1),
        ],
        axis=0,
    )
    identity = (
        lax.broadcasted_iota(jnp.int32, (members, members), 0)
        == lax.broadcasted_iota(jnp.int32, (members, members), 1)
    ).astype(jnp.float32)
    iterate = system / frobenius
    correction = split(1.5 * identity - 0.5 * iterate)
    z_high[...], z_low[...] = correction
    y_high[...], y_low[...] = split(product(split(iterate), correction))

    def sweep(index, carry):
        y = (y_high[...], y_low[...])
        z = (z_high[...], z_low[...])
        correction = split(1.5 * identity - 0.5 * product(z, y))
        y_high[...], y_low[...] = split(product(y, correction))
        z_high[...], z_low[...] = split(product(correction, z))
        return carry

    lax.fori_loop(1, ITERS - 1, sweep, 0)
    z = (z_high[...], z_low[...])
    correction = split(1.5 * identity - 0.5 * product(z, (y_high[...], y_low[...])))
    inverse_root = product(correction, z)
    root = split(inverse_root)
    driven = jnp.concatenate(
        [
            jnp.broadcast_to(total[3 * half : 3 * half + 1], (half, half)).T,
            jnp.broadcast_to(total[3 * half + 4 : 3 * half + 5], (half, half)).T,
        ],
        axis=0,
    )
    inner = product(root, split(driven))
    mean = product(root, split(inner)) / frobenius
    mixing = (
        inverse_root * jnp.sqrt((members - 1.0) / frobenius)
        + jnp.concatenate([mean, mean], axis=1)
    ).astype(jnp.bfloat16)
    mixed = lax.dot_general(
        mixing, anomaly[...], (((0,), (0,)), ((), ())), preferred_element_type=jnp.float32
    )
    analysed[...] = (center + mixed).astype(jnp.bfloat16).reshape(analysed.shape)
    for step in range(1, rows):
        analysis_copy(step).start()
    out_ref[row] = analysed[row]

    for part in range(3):
        across(part).wait_send()
        relay(part).wait_send()

    @pl.when(row < rows - 1)
    def _():
        coef_copy(True).wait_send()
        for part in range(3):
            sum_copy(True, part).wait_send()

    @pl.when(row > 0)
    def _():
        coef_copy(False).wait_send()
        for part in range(3):
            sum_copy(False, part).wait_send()

    for step in range(1, rows):
        forecast_copy(step).wait_send()
    for step in range(1, rows):
        analysis_copy(step).wait()


def solution(mesh):
    rows, cols = mesh.shape["mem"], mesh.shape["pat"]

    def on_device(states, spreads, innov, rinv, labels, lengths):
        share, _, _, state_len = states.shape
        obs, members = spreads.shape[2:]
        packed = 3 * (members // 2) + 8
        by_row = jnp.transpose(states.reshape(share, rows, state_len), (1, 0, 2))
        vmem = pl.BlockSpec(memory_space=pltpu.VMEM)
        dma = pltpu.SemaphoreType.DMA
        half = members // 2
        square = pltpu.VMEM((members, members), jnp.bfloat16)
        out = pl.pallas_call(
            functools.partial(kernel, rows, cols),
            out_shape=jax.ShapeDtypeStruct((rows, share, state_len), jnp.bfloat16),
            in_specs=[vmem] * 6,
            out_specs=vmem,
            scratch_shapes=[
                pltpu.VMEM((rows, share, state_len), jnp.bfloat16),
                pltpu.VMEM((3, packed, half), jnp.float32),
                pltpu.VMEM((3, 16, half), jnp.float32),
                pltpu.VMEM((2, packed, half), jnp.float32),
                pltpu.VMEM((2, packed, half), jnp.float32),
                pltpu.VMEM((packed, half), jnp.float32),
                square,
                square,
                square,
                square,
                pltpu.VMEM((members, state_len), jnp.bfloat16),
                pltpu.VMEM((rows, share, state_len), jnp.bfloat16),
                dma((rows,)),
                dma((rows,)),
                dma((3,)),
                dma((3,)),
                dma((3,)),
                dma((3,)),
                dma((2,)),
                dma((2,)),
                dma((2, 3)),
                dma((2, 3)),
                dma((rows,)),
                dma((rows,)),
            ],
            compiler_params=pltpu.CompilerParams(collective_id=0, has_side_effects=True),
        )(
            by_row,
            spreads.reshape(obs, members),
            innov.reshape(1, 1, obs),
            rinv.reshape(1, 1, obs),
            labels,
            lengths,
        )
        return jnp.transpose(out, (1, 0, 2)).reshape(states.shape)

    placed = (
        P("mem", None, "pat", None),
        P("mem", "pat", None, None),
        P("mem", "pat", None),
        P("mem", "pat", None),
        P("mem", "pat", None),
        P("mem", "pat"),
    )
    return jax.shard_map(
        on_device,
        mesh=mesh,
        in_specs=placed,
        out_specs=P("mem", None, "pat", None),
        check_vma=False,
    )
```

```python
import functools

import jax
import jax.numpy as jnp
from jax import lax
from jax.experimental import pallas as pl
from jax.experimental.pallas import tpu as pltpu
from jax.sharding import PartitionSpec as P

ITERS = 12


def split(value):
    high = value.astype(jnp.bfloat16)
    low = (value - high.astype(jnp.float32)).astype(jnp.bfloat16)
    return high, low


def product(left, right):
    return jnp.dot(
        jnp.concatenate([left[1], left[0], left[0]], axis=1),
        jnp.concatenate([right[0], right[1], right[0]], axis=0),
        preferred_element_type=jnp.float32,
    )


def left_product(left, right):
    return jnp.dot(
        jnp.concatenate(left, axis=1),
        jnp.concatenate([right.astype(jnp.bfloat16)] * 2, axis=0),
        preferred_element_type=jnp.float32,
    )


def right_product(left, right):
    return jnp.dot(
        jnp.concatenate([left.astype(jnp.bfloat16)] * 2, axis=1),
        jnp.concatenate(right, axis=0),
        preferred_element_type=jnp.float32,
    )


def store(full, high, low, value):
    full[...] = value
    high[...], low[...] = split(value)


def kernel(
    rows,
    cols,
    states_hbm,
    spreads_hbm,
    innov_ref,
    rinv_ref,
    labels_ref,
    length_ref,
    out_ref,
    states,
    spreads_ref,
    widened,
    states_ref,
    gathered,
    forecast,
    grams,
    coefs,
    sums,
    arrived,
    total,
    y_high,
    y_low,
    z_high,
    z_low,
    y_full,
    z_full,
    anomaly,
    analysed,
    fsend,
    frecv,
    gsend,
    grecv,
    ysend,
    yrecv,
    csend,
    crecv,
    ssend,
    srecv,
    osend,
    orecv,
    local,
):
    row = lax.axis_index("mem")
    col = lax.axis_index("pat")
    odd = lax.rem(col, 2)
    partner = col + 1 - 2 * odd
    onward = lax.rem(col + 2 - 4 * odd + cols, cols)
    behind = lax.rem(col - 2 + 4 * odd + cols, cols)
    members = forecast.shape[0] * forecast.shape[1]
    half = members // 2
    step_rows = half // 2
    chunks = tuple(
        (start, step_rows + (8 if start == 3 * half - step_rows else 0))
        for start in range(0, 3 * half, step_rows)
    )
    parts = len(chunks)

    barrier = pltpu.get_barrier_semaphore()
    pat_peers = [partner, onward] + ([behind] if cols > 4 else [])
    for peer in pat_peers:
        pl.semaphore_signal(barrier, 1, device_id={"pat": peer})

    for step in range(1, rows):
        pl.semaphore_signal(barrier, 1, device_id={"mem": lax.rem(row + step, rows)})

    load_spreads = pltpu.make_async_copy(spreads_hbm, spreads_ref, local.at[0])
    load_spreads.start()
    load_states = pltpu.make_async_copy(states_hbm, states, local.at[1])
    load_states.start()

    slot = lax.broadcasted_iota(jnp.int32, (16, labels_ref.shape[2]), 1)
    code = lax.broadcasted_iota(jnp.int32, (16, labels_ref.shape[2]), 0)
    used = (labels_ref[0] == code) & (slot < length_ref[...])
    shift_row = code // 3 - 1
    shift_col = code % 3 - 1
    distance = (shift_row * shift_row + shift_col * shift_col).astype(jnp.float32)
    coefficient = jnp.sum(
        jnp.where(used, jnp.exp(-0.5 * distance), 0.0), axis=1, keepdims=True
    )
    coefs[1] = jnp.broadcast_to(coefficient, coefs.shape[1:])

    load_spreads.wait()
    block = spreads_ref[...]
    weight = rinv_ref[0].astype(jnp.float32)
    scaled = jnp.concatenate(split(block.astype(jnp.float32).T * weight), axis=1)
    twice = jnp.concatenate([block, block], axis=0)
    upper = jnp.dot(scaled[:half], twice, preferred_element_type=jnp.float32)
    lower = jnp.dot(scaled[half:], twice[:, half:], preferred_element_type=jnp.float32)
    grams[0, 0:half] = upper[:, :half]
    grams[0, half : 2 * half] = upper[:, half:]
    grams[0, 2 * half : 3 * half] = lower
    weighted = split(weight * innov_ref[0].astype(jnp.float32))
    drive = jnp.dot(
        jnp.broadcast_to(jnp.concatenate(weighted, axis=1), (16, 2 * weight.shape[1])),
        twice,
        preferred_element_type=jnp.float32,
    )
    grams[0, 3 * half : 3 * half + 8] = jnp.concatenate(
        [drive[0:4, :half], drive[0:4, half:]], axis=0
    )
    pl.semaphore_wait(barrier, len(pat_peers) + rows - 1)

    def across(part):
        start, size = chunks[part]
        return pltpu.make_async_remote_copy(
            src_ref=grams.at[0, pl.ds(start, size)],
            dst_ref=grams.at[1, pl.ds(start, size)],
            send_sem=gsend.at[part],
            recv_sem=grecv.at[part],
            device_id={"pat": partner},
        )

    def relay(part):
        start, size = chunks[part]
        return pltpu.make_async_remote_copy(
            src_ref=grams.at[1, pl.ds(start, size)],
            dst_ref=grams.at[2, pl.ds(start, size)],
            send_sem=ysend.at[part],
            recv_sem=yrecv.at[part],
            device_id={"pat": onward},
        )

    def coef_copy(up):
        return pltpu.make_async_remote_copy(
            src_ref=coefs.at[1],
            dst_ref=coefs.at[0 if up else 2],
            send_sem=csend.at[0 if up else 1],
            recv_sem=crecv.at[0 if up else 1],
            device_id={"mem": row + 1 if up else row - 1},
        )

    def sum_copy(up, part):
        start, size = chunks[part]
        side = 0 if up else 1
        return pltpu.make_async_remote_copy(
            src_ref=sums.at[side, pl.ds(start, size)],
            dst_ref=arrived.at[side, pl.ds(start, size)],
            send_sem=ssend.at[side, part],
            recv_sem=srecv.at[side, part],
            device_id={"mem": row + 1 if up else row - 1},
        )

    def forecast_copy(step):
        peer = lax.rem(row + step, rows)
        return pltpu.make_async_remote_copy(
            src_ref=states_ref.at[peer],
            dst_ref=forecast.at[row],
            send_sem=fsend.at[step],
            recv_sem=frecv.at[step],
            device_id={"mem": peer},
        )

    def analysis_copy(step):
        peer = lax.rem(row + step, rows)
        return pltpu.make_async_remote_copy(
            src_ref=analysed.at[peer],
            dst_ref=gathered.at[row],
            send_sem=osend.at[step],
            recv_sem=orecv.at[step],
            device_id={"mem": peer},
        )

    for part in range(parts):
        across(part).start()

    @pl.when(row < rows - 1)
    def _():
        coef_copy(True).start()

    @pl.when(row > 0)
    def _():
        coef_copy(False).start()

    load_states.wait()
    share, state_len = states_ref.shape[1:]
    lanes = widened.shape[2]
    tiles = [slice(at, at + lanes) for at in range(0, state_len, lanes)]
    for tile, where in enumerate(tiles):
        wide = states[:, :, where].astype(jnp.float32)
        widened[tile] = wide.reshape(widened.shape[1:])
    for other in range(rows):
        for tile, where in enumerate(tiles):
            piece = widened[tile, pl.ds(other, share, stride=rows), :]
            states_ref[other, :, where] = piece.astype(jnp.bfloat16)
    forecast[row] = states_ref[row]

    for step in range(1, rows):
        forecast_copy(step).start()

    for part in range(parts):
        across(part).wait_recv()
        relay(part).start()

    @pl.when(row > 0)
    def _():
        coef_copy(True).wait_recv()

    @pl.when(row < rows - 1)
    def _():
        coef_copy(False).wait_recv()

    def combined(target, first, start, size):
        own = coefs[target, pl.ds(first + 1, 1), :]
        near = coefs[target, pl.ds(first + 2 - 2 * odd, 1), :]
        far = coefs[target, pl.ds(first + 2 * odd, 1), :]
        piece = pl.ds(start, size)
        return own * grams[0, piece] + near * grams[1, piece] + far * grams[2, piece]

    for part in range(parts):
        relay(part).wait_recv()
        start, size = chunks[part]

        @pl.when(row < rows - 1)
        def _():
            sums[0, pl.ds(start, size)] = combined(2, 0, start, size)
            sum_copy(True, part).start()

        @pl.when(row > 0)
        def _():
            sums[1, pl.ds(start, size)] = combined(0, 6, start, size)
            sum_copy(False, part).start()

        total[pl.ds(start, size)] = combined(1, 3, start, size)

    for step in range(1, rows):
        forecast_copy(step).wait_recv()
    values = forecast[...].reshape(members, forecast.shape[2]).astype(jnp.float32)
    center = jnp.sum(values, axis=0, keepdims=True) * (1.0 / members)
    anomaly[...] = (values - center).astype(jnp.bfloat16)

    for part in range(parts):
        start, size = chunks[part]

        @pl.when(row > 0)
        def _():
            sum_copy(True, part).wait_recv()
            total[pl.ds(start, size)] += arrived[0, pl.ds(start, size)]

        @pl.when(row < rows - 1)
        def _():
            sum_copy(False, part).wait_recv()
            total[pl.ds(start, size)] += arrived[1, pl.ds(start, size)]

    eye_half = (
        lax.broadcasted_iota(jnp.int32, (half, half), 0)
        == lax.broadcasted_iota(jnp.int32, (half, half), 1)
    ).astype(jnp.float32)
    first = total[0:half] + (members - 1.0) * eye_half
    cross = total[half : 2 * half]
    last = total[2 * half : 3 * half] + (members - 1.0) * eye_half
    squares = first * first + 2.0 * (cross * cross) + last * last
    frobenius = jnp.sqrt(
        jnp.sum(jnp.sum(squares, axis=0, keepdims=True), axis=1, keepdims=True)
    )
    system = jnp.concatenate(
        [
            jnp.concatenate([first, cross], axis=1),
            jnp.concatenate([cross.T, last], axis=1),
        ],
        axis=0,
    )
    identity = (
        lax.broadcasted_iota(jnp.int32, (members, members), 0)
        == lax.broadcasted_iota(jnp.int32, (members, members), 1)
    ).astype(jnp.float32)
    iterate = system / frobenius
    change = 0.5 * (identity - iterate)
    store(z_full, z_high, z_low, identity + change)
    store(y_full, y_high, y_low, iterate + left_product(split(iterate), change))

    def sweep(exact, index, carry):
        if exact:
            near_identity = product((z_high[...], z_low[...]), (y_high[...], y_low[...]))
        else:
            near_identity = jnp.dot(
                z_high[...], y_high[...], preferred_element_type=jnp.float32
            )
        change = 0.5 * (identity - near_identity)
        y = y_full[...] + left_product((y_high[...], y_low[...]), change)
        z = z_full[...] + right_product(change, (z_high[...], z_low[...]))
        store(y_full, y_high, y_low, y)
        store(z_full, z_high, z_low, z)
        return carry

    lax.fori_loop(1, ITERS - 3, functools.partial(sweep, False), 0)
    lax.fori_loop(ITERS - 3, ITERS - 1, functools.partial(sweep, True), 0)
    z = (z_high[...], z_low[...])
    change = 0.5 * (identity - product(z, (y_high[...], y_low[...])))
    inverse_root = z_full[...] + right_product(change, z)
    root = split(inverse_root)
    driven = jnp.concatenate(
        [
            jnp.broadcast_to(total[3 * half : 3 * half + 1], (half, half)).T,
            jnp.broadcast_to(total[3 * half + 4 : 3 * half + 5], (half, half)).T,
        ],
        axis=0,
    )
    inner = product(root, split(driven))
    mean = product(root, split(inner)) / frobenius
    mixing = (
        inverse_root * jnp.sqrt((members - 1.0) / frobenius)
        + jnp.concatenate([mean, mean], axis=1)
    ).astype(jnp.bfloat16)
    mixed = lax.dot_general(
        mixing, anomaly[...], (((0,), (0,)), ((), ())), preferred_element_type=jnp.float32
    )
    analysed[...] = (center + mixed).astype(jnp.bfloat16).reshape(analysed.shape)
    for step in range(1, rows):
        analysis_copy(step).start()

    def place(source, other):
        wide = source.astype(jnp.float32)
        for tile, where in enumerate(tiles):
            widened[tile, pl.ds(other, share, stride=rows), :] = wide[:, where]

    place(analysed[row], row)
    for step in range(1, rows):
        analysis_copy(step).wait_recv()
        giver = lax.rem(row - step + rows, rows)
        place(gathered[giver], giver)
    for tile, where in enumerate(tiles):
        shape = (share, rows, lanes)
        out_ref[:, :, where] = widened[tile].reshape(shape).astype(jnp.bfloat16)

    for part in range(parts):
        across(part).wait_send()
        relay(part).wait_send()

    @pl.when(row < rows - 1)
    def _():
        coef_copy(True).wait_send()
        for part in range(parts):
            sum_copy(True, part).wait_send()

    @pl.when(row > 0)
    def _():
        coef_copy(False).wait_send()
        for part in range(parts):
            sum_copy(False, part).wait_send()

    for step in range(1, rows):
        forecast_copy(step).wait_send()
    for step in range(1, rows):
        analysis_copy(step).wait_send()


def solution(mesh):
    rows, cols = mesh.shape["mem"], mesh.shape["pat"]

    def on_device(states, spreads, innov, rinv, labels, lengths):
        share, _, _, state_len = states.shape
        obs, members = spreads.shape[2:]
        packed = 3 * (members // 2) + 8
        parts = 6
        vmem = pl.BlockSpec(memory_space=pltpu.VMEM)
        dma = pltpu.SemaphoreType.DMA
        half = members // 2
        square = pltpu.VMEM((members, members), jnp.bfloat16)
        out = pl.pallas_call(
            functools.partial(kernel, rows, cols),
            out_shape=jax.ShapeDtypeStruct((share, rows, state_len), jnp.bfloat16),
            in_specs=[pl.BlockSpec(memory_space=pl.ANY)] * 2 + [vmem] * 4,
            out_specs=vmem,
            scratch_shapes=[
                pltpu.VMEM((share, rows, state_len), jnp.bfloat16),
                pltpu.VMEM((obs, members), jnp.bfloat16),
                pltpu.VMEM((state_len // half, share * rows, half), jnp.float32),
                pltpu.VMEM((rows, share, state_len), jnp.bfloat16),
                pltpu.VMEM((rows, share, state_len), jnp.bfloat16),
                pltpu.VMEM((rows, share, state_len), jnp.bfloat16),
                pltpu.VMEM((3, packed, half), jnp.float32),
                pltpu.VMEM((3, 16, half), jnp.float32),
                pltpu.VMEM((2, packed, half), jnp.float32),
                pltpu.VMEM((2, packed, half), jnp.float32),
                pltpu.VMEM((packed, half), jnp.float32),
                square,
                square,
                square,
                square,
                pltpu.VMEM((members, members), jnp.float32),
                pltpu.VMEM((members, members), jnp.float32),
                pltpu.VMEM((members, state_len), jnp.bfloat16),
                pltpu.VMEM((rows, share, state_len), jnp.bfloat16),
                dma((rows,)),
                dma((rows,)),
                dma((parts,)),
                dma((parts,)),
                dma((parts,)),
                dma((parts,)),
                dma((2,)),
                dma((2,)),
                dma((2, parts)),
                dma((2, parts)),
                dma((rows,)),
                dma((rows,)),
                dma((2,)),
            ],
            compiler_params=pltpu.CompilerParams(collective_id=0, has_side_effects=True),
        )(
            states.reshape(share, rows, state_len),
            spreads.reshape(obs, members),
            innov.reshape(1, 1, obs),
            rinv.reshape(1, 1, obs),
            labels,
            lengths,
        )
        return out.reshape(states.shape)

    placed = (
        P("mem", None, "pat", None),
        P("mem", "pat", None, None),
        P("mem", "pat", None),
        P("mem", "pat", None),
        P("mem", "pat", None),
        P("mem", "pat"),
    )
    return jax.shard_map(
        on_device,
        mesh=mesh,
        in_specs=placed,
        out_specs=P("mem", None, "pat", None),
        check_vma=False,
    )
```

```python
import functools

import jax
import jax.numpy as jnp
from jax import lax
from jax.experimental import pallas as pl
from jax.experimental.pallas import tpu as pltpu
from jax.sharding import PartitionSpec as P

ITERS = 12


def split(value):
    high = value.astype(jnp.bfloat16)
    low = (value - high.astype(jnp.float32)).astype(jnp.bfloat16)
    return high, low


def product(left, right):
    return jnp.dot(
        jnp.concatenate([left[1], left[0], left[0]], axis=1),
        jnp.concatenate([right[0], right[1], right[0]], axis=0),
        preferred_element_type=jnp.float32,
    )


def left_product(left, right):
    both = jnp.dot(
        jnp.concatenate(left, axis=0),
        right.astype(jnp.bfloat16),
        preferred_element_type=jnp.float32,
    )
    return both[: right.shape[0]] + both[right.shape[0] :]


def right_product(left, right):
    both = jnp.dot(
        left.astype(jnp.bfloat16),
        jnp.concatenate(right, axis=1),
        preferred_element_type=jnp.float32,
    )
    return both[:, : left.shape[1]] + both[:, left.shape[1] :]


def store(full, high, low, value):
    full[...] = value
    high[...], low[...] = split(value)


def kernel(
    rows,
    cols,
    states_hbm,
    spreads_hbm,
    innov_ref,
    rinv_ref,
    labels_ref,
    length_ref,
    out_ref,
    states,
    spreads_ref,
    widened,
    states_ref,
    gathered,
    forecast,
    grams,
    coefs,
    sums,
    arrived,
    total,
    y_high,
    y_low,
    z_high,
    z_low,
    y_full,
    z_full,
    anomaly,
    analysed,
    fsend,
    frecv,
    gsend,
    grecv,
    ysend,
    yrecv,
    csend,
    crecv,
    ssend,
    srecv,
    osend,
    orecv,
    local,
):
    row = lax.axis_index("mem")
    col = lax.axis_index("pat")
    odd = lax.rem(col, 2)
    partner = col + 1 - 2 * odd
    onward = lax.rem(col + 2 - 4 * odd + cols, cols)
    behind = lax.rem(col - 2 + 4 * odd + cols, cols)
    members = forecast.shape[0] * forecast.shape[1]
    half = members // 2
    step_rows = half // 2
    chunks = tuple(
        (start, step_rows + (8 if start == 3 * half - step_rows else 0))
        for start in range(0, 3 * half, step_rows)
    )
    parts = len(chunks)

    barrier = pltpu.get_barrier_semaphore()
    pat_peers = [partner, onward] + ([behind] if cols > 4 else [])
    for peer in pat_peers:
        pl.semaphore_signal(barrier, 1, device_id={"pat": peer})

    for step in range(1, rows):
        pl.semaphore_signal(barrier, 1, device_id={"mem": lax.rem(row + step, rows)})

    load_spreads = pltpu.make_async_copy(spreads_hbm, spreads_ref, local.at[0])
    load_spreads.start()
    load_states = pltpu.make_async_copy(states_hbm, states, local.at[1])
    load_states.start()

    slot = lax.broadcasted_iota(jnp.int32, (16, labels_ref.shape[2]), 1)
    code = lax.broadcasted_iota(jnp.int32, (16, labels_ref.shape[2]), 0)
    used = (labels_ref[0] == code) & (slot < length_ref[...])
    shift_row = code // 3 - 1
    shift_col = code % 3 - 1
    distance = (shift_row * shift_row + shift_col * shift_col).astype(jnp.float32)
    coefficient = jnp.sum(
        jnp.where(used, jnp.exp(-0.5 * distance), 0.0), axis=1, keepdims=True
    )
    coefs[1] = jnp.broadcast_to(coefficient, coefs.shape[1:])

    load_spreads.wait()
    block = spreads_ref[...]
    weight = rinv_ref[0].astype(jnp.float32)
    scaled = jnp.concatenate(split(block.astype(jnp.float32).T * weight), axis=1)
    twice = jnp.concatenate([block, block], axis=0)
    upper = jnp.dot(scaled[:half], twice, preferred_element_type=jnp.float32)
    lower = jnp.dot(scaled[half:], twice[:, half:], preferred_element_type=jnp.float32)
    grams[0, 0:half] = upper[:, :half]
    grams[0, half : 2 * half] = upper[:, half:]
    grams[0, 2 * half : 3 * half] = lower
    weighted = split(weight * innov_ref[0].astype(jnp.float32))
    drive = jnp.dot(
        jnp.broadcast_to(jnp.concatenate(weighted, axis=1), (16, 2 * weight.shape[1])),
        twice,
        preferred_element_type=jnp.float32,
    )
    grams[0, 3 * half : 3 * half + 8] = jnp.concatenate(
        [drive[0:4, :half], drive[0:4, half:]], axis=0
    )
    pl.semaphore_wait(barrier, len(pat_peers) + rows - 1)

    def across(part):
        start, size = chunks[part]
        return pltpu.make_async_remote_copy(
            src_ref=grams.at[0, pl.ds(start, size)],
            dst_ref=grams.at[1, pl.ds(start, size)],
            send_sem=gsend.at[part],
            recv_sem=grecv.at[part],
            device_id={"pat": partner},
        )

    def relay(part):
        start, size = chunks[part]
        return pltpu.make_async_remote_copy(
            src_ref=grams.at[1, pl.ds(start, size)],
            dst_ref=grams.at[2, pl.ds(start, size)],
            send_sem=ysend.at[part],
            recv_sem=yrecv.at[part],
            device_id={"pat": onward},
        )

    def coef_copy(up):
        return pltpu.make_async_remote_copy(
            src_ref=coefs.at[1],
            dst_ref=coefs.at[0 if up else 2],
            send_sem=csend.at[0 if up else 1],
            recv_sem=crecv.at[0 if up else 1],
            device_id={"mem": row + 1 if up else row - 1},
        )

    def sum_copy(up, part):
        start, size = chunks[part]
        side = 0 if up else 1
        return pltpu.make_async_remote_copy(
            src_ref=sums.at[side, pl.ds(start, size)],
            dst_ref=arrived.at[side, pl.ds(start, size)],
            send_sem=ssend.at[side, part],
            recv_sem=srecv.at[side, part],
            device_id={"mem": row + 1 if up else row - 1},
        )

    def forecast_copy(step):
        peer = lax.rem(row + step, rows)
        return pltpu.make_async_remote_copy(
            src_ref=states_ref.at[peer],
            dst_ref=forecast.at[row],
            send_sem=fsend.at[step],
            recv_sem=frecv.at[step],
            device_id={"mem": peer},
        )

    def analysis_copy(step):
        peer = lax.rem(row + step, rows)
        return pltpu.make_async_remote_copy(
            src_ref=analysed.at[peer],
            dst_ref=gathered.at[row],
            send_sem=osend.at[step],
            recv_sem=orecv.at[step],
            device_id={"mem": peer},
        )

    for part in range(parts):
        across(part).start()

    @pl.when(row < rows - 1)
    def _():
        coef_copy(True).start()

    @pl.when(row > 0)
    def _():
        coef_copy(False).start()

    load_states.wait()
    share, state_len = states_ref.shape[1:]
    lanes = widened.shape[2]
    tiles = [slice(at, at + lanes) for at in range(0, state_len, lanes)]
    for tile, where in enumerate(tiles):
        wide = states[:, :, where].astype(jnp.float32)
        widened[tile] = wide.reshape(widened.shape[1:])
    for other in range(rows):
        for tile, where in enumerate(tiles):
            piece = widened[tile, pl.ds(other, share, stride=rows), :]
            states_ref[other, :, where] = piece.astype(jnp.bfloat16)
    forecast[row] = states_ref[row]

    for step in range(1, rows):
        forecast_copy(step).start()

    for part in range(parts):
        across(part).wait_recv()
        relay(part).start()

    @pl.when(row > 0)
    def _():
        coef_copy(True).wait_recv()

    @pl.when(row < rows - 1)
    def _():
        coef_copy(False).wait_recv()

    def combined(target, first, start, size):
        own = coefs[target, pl.ds(first + 1, 1), :]
        near = coefs[target, pl.ds(first + 2 - 2 * odd, 1), :]
        far = coefs[target, pl.ds(first + 2 * odd, 1), :]
        piece = pl.ds(start, size)
        return own * grams[0, piece] + near * grams[1, piece] + far * grams[2, piece]

    for part in range(parts):
        relay(part).wait_recv()
        start, size = chunks[part]

        @pl.when(row < rows - 1)
        def _():
            sums[0, pl.ds(start, size)] = combined(2, 0, start, size)
            sum_copy(True, part).start()

        @pl.when(row > 0)
        def _():
            sums[1, pl.ds(start, size)] = combined(0, 6, start, size)
            sum_copy(False, part).start()

        total[pl.ds(start, size)] = combined(1, 3, start, size)

    for step in range(1, rows):
        forecast_copy(step).wait_recv()
    values = forecast[...].reshape(members, forecast.shape[2]).astype(jnp.float32)
    center = jnp.sum(values, axis=0, keepdims=True) * (1.0 / members)
    anomaly[...] = (values - center).astype(jnp.bfloat16)

    for part in range(parts):
        start, size = chunks[part]

        @pl.when(row > 0)
        def _():
            sum_copy(True, part).wait_recv()
            total[pl.ds(start, size)] += arrived[0, pl.ds(start, size)]

        @pl.when(row < rows - 1)
        def _():
            sum_copy(False, part).wait_recv()
            total[pl.ds(start, size)] += arrived[1, pl.ds(start, size)]

    eye_half = (
        lax.broadcasted_iota(jnp.int32, (half, half), 0)
        == lax.broadcasted_iota(jnp.int32, (half, half), 1)
    ).astype(jnp.float32)
    first = total[0:half] + (members - 1.0) * eye_half
    cross = total[half : 2 * half]
    last = total[2 * half : 3 * half] + (members - 1.0) * eye_half
    squares = first * first + 2.0 * (cross * cross) + last * last
    frobenius = jnp.sqrt(
        jnp.sum(jnp.sum(squares, axis=0, keepdims=True), axis=1, keepdims=True)
    )
    system = jnp.concatenate(
        [
            jnp.concatenate([first, cross], axis=1),
            jnp.concatenate([cross.T, last], axis=1),
        ],
        axis=0,
    )
    identity = (
        lax.broadcasted_iota(jnp.int32, (members, members), 0)
        == lax.broadcasted_iota(jnp.int32, (members, members), 1)
    ).astype(jnp.float32)
    iterate = system / frobenius
    change = 0.5 * (identity - iterate)
    store(z_full, z_high, z_low, identity + change)
    store(y_full, y_high, y_low, iterate + left_product(split(iterate), change))

    def sweep(index, carry):
        near_identity = jnp.dot(
            z_high[...], y_high[...], preferred_element_type=jnp.float32
        )
        change = 0.5 * (identity - near_identity)
        y = y_full[...] + left_product((y_high[...], y_low[...]), change)
        z = z_full[...] + right_product(change, (z_high[...], z_low[...]))
        store(y_full, y_high, y_low, y)
        store(z_full, z_high, z_low, z)
        return carry

    lax.fori_loop(1, ITERS - 1, sweep, 0)
    z = (z_high[...], z_low[...])
    change = 0.5 * (identity - product(z, (y_high[...], y_low[...])))
    inverse_root = z_full[...] + right_product(change, z)
    root = split(inverse_root)
    driven = jnp.concatenate(
        [
            jnp.broadcast_to(total[3 * half : 3 * half + 1], (half, half)).T,
            jnp.broadcast_to(total[3 * half + 4 : 3 * half + 5], (half, half)).T,
        ],
        axis=0,
    )
    inner = product(root, split(driven))
    mean = product(root, split(inner)) / frobenius
    mixing = (
        inverse_root * jnp.sqrt((members - 1.0) / frobenius)
        + jnp.concatenate([mean, mean], axis=1)
    ).astype(jnp.bfloat16)
    mixed = lax.dot_general(
        mixing, anomaly[...], (((0,), (0,)), ((), ())), preferred_element_type=jnp.float32
    )
    analysed[...] = (center + mixed).astype(jnp.bfloat16).reshape(analysed.shape)
    for step in range(1, rows):
        analysis_copy(step).start()

    def place(source, other):
        wide = source.astype(jnp.float32)
        for tile, where in enumerate(tiles):
            widened[tile, pl.ds(other, share, stride=rows), :] = wide[:, where]

    place(analysed[row], row)
    for step in range(1, rows):
        analysis_copy(step).wait_recv()
        giver = lax.rem(row - step + rows, rows)
        place(gathered[giver], giver)
    for tile, where in enumerate(tiles):
        shape = (share, rows, lanes)
        out_ref[:, :, where] = widened[tile].reshape(shape).astype(jnp.bfloat16)

    for part in range(parts):
        across(part).wait_send()
        relay(part).wait_send()

    @pl.when(row < rows - 1)
    def _():
        coef_copy(True).wait_send()
        for part in range(parts):
            sum_copy(True, part).wait_send()

    @pl.when(row > 0)
    def _():
        coef_copy(False).wait_send()
        for part in range(parts):
            sum_copy(False, part).wait_send()

    for step in range(1, rows):
        forecast_copy(step).wait_send()
    for step in range(1, rows):
        analysis_copy(step).wait_send()


def solution(mesh):
    rows, cols = mesh.shape["mem"], mesh.shape["pat"]

    def on_device(states, spreads, innov, rinv, labels, lengths):
        share, _, _, state_len = states.shape
        obs, members = spreads.shape[2:]
        packed = 3 * (members // 2) + 8
        parts = 6
        vmem = pl.BlockSpec(memory_space=pltpu.VMEM)
        dma = pltpu.SemaphoreType.DMA
        half = members // 2
        square = pltpu.VMEM((members, members), jnp.bfloat16)
        out = pl.pallas_call(
            functools.partial(kernel, rows, cols),
            out_shape=jax.ShapeDtypeStruct((share, rows, state_len), jnp.bfloat16),
            in_specs=[pl.BlockSpec(memory_space=pl.ANY)] * 2 + [vmem] * 4,
            out_specs=vmem,
            scratch_shapes=[
                pltpu.VMEM((share, rows, state_len), jnp.bfloat16),
                pltpu.VMEM((obs, members), jnp.bfloat16),
                pltpu.VMEM((state_len // half, share * rows, half), jnp.float32),
                pltpu.VMEM((rows, share, state_len), jnp.bfloat16),
                pltpu.VMEM((rows, share, state_len), jnp.bfloat16),
                pltpu.VMEM((rows, share, state_len), jnp.bfloat16),
                pltpu.VMEM((3, packed, half), jnp.float32),
                pltpu.VMEM((3, 16, half), jnp.float32),
                pltpu.VMEM((2, packed, half), jnp.float32),
                pltpu.VMEM((2, packed, half), jnp.float32),
                pltpu.VMEM((packed, half), jnp.float32),
                square,
                square,
                square,
                square,
                pltpu.VMEM((members, members), jnp.float32),
                pltpu.VMEM((members, members), jnp.float32),
                pltpu.VMEM((members, state_len), jnp.bfloat16),
                pltpu.VMEM((rows, share, state_len), jnp.bfloat16),
                dma((rows,)),
                dma((rows,)),
                dma((parts,)),
                dma((parts,)),
                dma((parts,)),
                dma((parts,)),
                dma((2,)),
                dma((2,)),
                dma((2, parts)),
                dma((2, parts)),
                dma((rows,)),
                dma((rows,)),
                dma((2,)),
            ],
            compiler_params=pltpu.CompilerParams(collective_id=0, has_side_effects=True),
        )(
            states.reshape(share, rows, state_len),
            spreads.reshape(obs, members),
            innov.reshape(1, 1, obs),
            rinv.reshape(1, 1, obs),
            labels,
            lengths,
        )
        return out.reshape(states.shape)

    placed = (
        P("mem", None, "pat", None),
        P("mem", "pat", None, None),
        P("mem", "pat", None),
        P("mem", "pat", None),
        P("mem", "pat", None),
        P("mem", "pat"),
    )
    return jax.shard_map(
        on_device,
        mesh=mesh,
        in_specs=placed,
        out_specs=P("mem", None, "pat", None),
        check_vma=False,
    )
```
